32 devices in a mesh: row: 8 (over z, y), col: 4 (over x, core).
Axes of the slice: x: 2, y: 2, z: 4, core: 2. Of those that a mesh axis runs over, the one named last changes fastest.
Arguments:
- tokens: bfloat16 [384, 8192], P('row', 'col'), may hold values from -6 to 6
- weight: bfloat16 [8192, 32768], P('col', 'row'), may hold values from -0.109375 to 0.109375
- tile_rows: int32 [8, 4, 256], P('row', 'col'), may hold values from 0 to 63, as said below
- tile_cols: int32 [8, 4, 256], P('row', 'col'), may hold values from 0 to 255, as said below
- tile_count: int32 [8, 4], P('row', 'col'), may hold values from 64 to 256, as said below
- hidden_cotangent: bfloat16 [384, 32768], P('col', 'row'), may hold values from -6 to 6
Outputs:
- hidden: bfloat16 [384, 32768], P('col', 'row')
- input_grad: bfloat16 [384, 8192], P('row', 'col')
- weight_grad: bfloat16 [8192, 32768], P('col', 'row')
The draws below stay inside these ranges and needn't reach their ends.
Inputs may be any that keep to these rules, and one draw needn't show every extreme that they name: tile_rows[r, c, k] is a row block of the weight (tiles of 128 x 128) among the 16 blocks from c * 16 on, which index c of col holds. tile_cols[r, c, k] is a column block among the 32 blocks from r * 32 on, which index r of row holds; the 256 candidate tiles of one device are distinct. The first tile_count[r, c] candidates of device (r, c) are its nonzero tiles; some device holds 256.
All inputs are finite; a program needn't handle non-finite values.
Results may differ from the reference program's by a relative error of at most 0.0049.
Values may be sent and summed in bfloat16 or wider, within the bound.
A program may use at most 128 MiB of HBM per device.

```python
import jax
import jax.numpy as jnp

D = 8192
FF = 32768
TILE = 128
TOKENS = 384
RBD = 16
CBD = 32
BLOCKS_DEV = 512
CAP = 256
N_ROW = 8
N_COL = 4


def tile_slots(key):
    scores = jax.random.randint(jax.random.fold_in(key, 7), (N_ROW, N_COL, BLOCKS_DEV), 0, 2 ** 20)
    scores = scores * BLOCKS_DEV + jnp.arange(BLOCKS_DEV, dtype=jnp.int32)
    ordering = jnp.argsort(scores, axis=-1, stable=True)
    return ordering[:, :, :CAP].astype(jnp.int32)


def draw_tile_rows(key, part):
    slots = tile_slots(key)
    offset = (jnp.arange(N_COL, dtype=jnp.int32) * RBD)[None, :, None]
    return (offset + slots // CBD).astype(jnp.int32)


def draw_tile_cols(key, part):
    slots = tile_slots(key)
    offset = (jnp.arange(N_ROW, dtype=jnp.int32) * CBD)[:, None, None]
    return (offset + slots % CBD).astype(jnp.int32)


def draw_tile_count(key, part):
    counts = jax.random.randint(jax.random.fold_in(key, 11), (N_ROW, N_COL), CAP // 4, CAP + 1)
    chosen = jax.random.randint(jax.random.fold_in(key, 13), (), 0, N_ROW * N_COL)
    flat_index = jnp.arange(N_ROW * N_COL, dtype=jnp.int32).reshape(N_ROW, N_COL)
    return jnp.where(flat_index == chosen, CAP, counts).astype(jnp.int32)


def steps_of(key, dims, cuts, least, high):
    level = 1.0
    for dim, blocks in cuts:
        steps = jax.random.uniform(jax.random.fold_in(jax.random.fold_in(key, 6), dim), (blocks,), jnp.float32, least / len(cuts), high / len(cuts))
        level = level * jnp.repeat(jnp.exp(steps), dims[dim] // blocks).reshape((-1,) + (1,) * (len(dims) - 1 - dim))
    return level


def noise(rng, dims, width, limit, split=(), kind=jnp.bfloat16):
    array = jax.random.normal(rng, dims, jnp.float32) * width
    if len(split) > 0:
        array = steps_of(rng, dims, split, -0.22, 0.18) * array
    return jnp.clip(array, min=-limit, max=limit).astype(kind)


def setup_inputs(seed: int = 0) -> dict:
    keys = jax.random.split(jax.random.key(seed), 7)
    tokens = noise(keys[0], (TOKENS, D), 1.0, 6.0, ((0, 8), (1, 4)))
    weight = noise(keys[1], (D, FF), (D // 3) ** -0.5, 0.109375, ((0, 4), (1, 8)))
    tile_rows = draw_tile_rows(jax.random.fold_in(keys[6], 71), 0)
    tile_cols = draw_tile_cols(jax.random.fold_in(keys[6], 71), 0)
    tile_count = draw_tile_count(jax.random.fold_in(keys[6], 71), 0)
    hidden_cotangent = noise(keys[5], (TOKENS, FF), 1.0, 6.0, ((0, 4), (1, 8)))
    return dict(tokens=tokens, weight=weight, tile_rows=tile_rows, tile_cols=tile_cols, tile_count=tile_count, hidden_cotangent=hidden_cotangent)


def reference(tokens, weight, tile_rows, tile_cols, tile_count, hidden_cotangent):
    row_list = tile_rows.reshape(-1).astype(jnp.int32)
    col_list = tile_cols.reshape(-1).astype(jnp.int32)
    is_live = (jnp.arange(CAP)[None, :] < tile_count.reshape(-1, 1)).reshape(-1).astype(jnp.float32)
    block_mask = jnp.zeros((D // TILE, FF // TILE), jnp.float32).at[row_list, col_list].max(is_live)
    dense_mask = jnp.repeat(jnp.repeat(block_mask.astype(jnp.bfloat16), TILE, 0), TILE, 1)
    masked = weight * dense_mask
    pre_act = jnp.dot(tokens, masked, preferred_element_type=jnp.float32)
    gate_value = jax.nn.sigmoid(pre_act)
    hidden = (pre_act * gate_value).astype(jnp.bfloat16)
    silu_slope = gate_value * (1.0 + pre_act * (1.0 - gate_value))
    grad_pre = (hidden_cotangent.astype(jnp.float32) * silu_slope).astype(jnp.bfloat16)
    input_grad = jnp.dot(grad_pre, masked.T, preferred_element_type=jnp.float32).astype(jnp.bfloat16)
    full_grad = jnp.dot(tokens.T, grad_pre, preferred_element_type=jnp.float32)
    weight_grad = jnp.where(dense_mask > 0, full_grad, jnp.zeros_like(full_grad)).astype(jnp.bfloat16)
    return hidden, input_grad, weight_grad
```

```python
import jax
import jax.numpy as jnp
from jax import lax
from jax.sharding import PartitionSpec as P

TILE = 128


def exchange_sum(partial, axis):
    n = lax.psum(1, axis)
    rows = partial.shape[0] // n
    mine = lax.all_to_all(
        partial.reshape(n, rows, partial.shape[1]), axis, split_axis=0, concat_axis=0
    )
    return mine.astype(jnp.float32).sum(axis=0)


def on_device(tokens, weight, tile_rows, tile_cols, tile_count, hidden_cotangent):
    row_index = lax.axis_index("row")
    col_index = lax.axis_index("col")
    row_blocks = weight.shape[0] // TILE
    col_blocks = weight.shape[1] // TILE
    capacity = tile_rows.shape[2]
    local_rows = tile_rows.reshape(capacity) - col_index * row_blocks
    local_cols = tile_cols.reshape(capacity) - row_index * col_blocks
    is_live = jnp.arange(capacity) < tile_count.reshape(())
    row_pick = (
        (local_rows[None, :] == jnp.arange(row_blocks)[:, None]) & is_live[None, :]
    ).astype(jnp.bfloat16)
    col_pick = (local_cols[:, None] == (jnp.arange(weight.shape[1]) // TILE)[None, :]).astype(
        jnp.bfloat16
    )
    mask = jnp.dot(row_pick, col_pick, preferred_element_type=jnp.float32)
    live = (mask > 0.5)[:, None, :]
    shaped = weight.reshape(row_blocks, TILE, weight.shape[1])
    masked = jnp.where(live, shaped, jnp.zeros_like(shaped)).reshape(weight.shape)

    full_tokens = lax.all_gather(tokens, "row", axis=0, tiled=True)
    partial = jnp.dot(full_tokens, masked, preferred_element_type=jnp.float32)
    pre_act = exchange_sum(partial.astype(jnp.bfloat16), "col")
    gate_value = jax.nn.sigmoid(pre_act)
    hidden = (pre_act * gate_value).astype(jnp.bfloat16)
    silu_slope = gate_value * (1.0 + pre_act * (1.0 - gate_value))
    grad_pre = (hidden_cotangent.astype(jnp.float32) * silu_slope).astype(jnp.bfloat16)
    full_grads = lax.all_gather(grad_pre, "col", axis=0, tiled=True)
    share = lax.dot_general(
        full_grads, masked, (((1,), (1,)), ((), ())), preferred_element_type=jnp.float32
    )
    input_grad = exchange_sum(share.astype(jnp.bfloat16), "row").astype(jnp.bfloat16)
    full = lax.dot_general(
        full_tokens, full_grads, (((0,), (0,)), ((), ())), preferred_element_type=jnp.float32
    ).reshape(row_blocks, TILE, weight.shape[1])
    weight_grad = jnp.where(live, full, 0.0).astype(jnp.bfloat16).reshape(weight.shape)
    return (hidden, input_grad, weight_grad)


def solution(mesh):
    in_specs = (
        P("row", "col"),
        P("col", "row"),
        P("row", "col", None),
        P("row", "col", None),
        P("row", "col"),
        P("col", "row"),
    )
    out_specs = (P("col", "row"), P("row", "col"), P("col", "row"))
    return jax.shard_map(
        on_device, mesh=mesh, in_specs=in_specs, out_specs=out_specs, check_vma=False
    )
```

```python
import jax
import jax.numpy as jnp
from jax import lax
from jax.experimental import pallas as pl
from jax.experimental.pallas import tpu as pltpu
from jax.sharding import PartitionSpec as P

TILE = 128


def exchange_sum(partial, axis):
    n = lax.psum(1, axis)
    rows = partial.shape[0] // n
    mine = lax.all_to_all(
        partial.reshape(n, rows, partial.shape[1]), axis, split_axis=0, concat_axis=0
    )
    return mine.astype(jnp.float32).sum(axis=0)


def paired_exchange_sum(partial, axis):
    n = lax.psum(1, axis)
    if n % 2:
        return exchange_sum(partial, axis)
    chips = n // 2
    rows = partial.shape[0] // n
    here = lax.axis_index(axis)
    chip, core = here // 2, here % 2
    blocks = partial.reshape(chips, 2, rows, partial.shape[1])
    away = lax.dynamic_index_in_dim(blocks, 1 - core, 1, keepdims=False)
    keep = lax.dynamic_index_in_dim(blocks, core, 1, keepdims=False)
    came = lax.ppermute(away, axis, [(i, i ^ 1) for i in range(n)])

    def pair_block(which):
        ours = lax.dynamic_index_in_dim(keep, which, 0, keepdims=False)
        theirs = lax.dynamic_index_in_dim(came, which, 0, keepdims=False)
        return ours.astype(jnp.float32) + theirs.astype(jnp.float32)

    arrived = [
        lax.ppermute(
            pair_block((chip + step) % chips).astype(jnp.bfloat16),
            axis,
            [(i, (i + 2 * step) % n) for i in range(n)],
        )
        for step in range(1, chips)
    ]
    total = pair_block(chip)
    for block in arrived:
        total = total + block.astype(jnp.float32)
    return total


def mask_weight(mask_ref, weight_ref, held):
    for block in range(mask_ref.shape[0]):
        rows = pl.ds(block * TILE, TILE)
        tile = weight_ref[rows, :]
        live = jnp.broadcast_to(mask_ref[block : block + 1, :], tile.shape) > 0.5
        held[rows, :] = jnp.where(live, tile.astype(jnp.float32), 0.0).astype(jnp.bfloat16)


def forward_kernel(mask_ref, tokens_ref, weight_ref, out_ref, held):
    mask_weight(mask_ref, weight_ref, held)
    out_ref[...] = jnp.dot(
        tokens_ref[...], held[...], preferred_element_type=jnp.float32
    ).astype(jnp.bfloat16)


def backward_kernel(mask_ref, grads_ref, weight_ref, out_ref, held, total):
    step = pl.program_id(0)
    mask_weight(mask_ref, weight_ref, held)
    product = lax.dot_general(
        grads_ref[...], held[...], (((1,), (1,)), ((), ())), preferred_element_type=jnp.float32
    )

    @pl.when(step == 0)
    def _():
        total[...] = product

    @pl.when(step > 0)
    def _():
        total[...] += product

    @pl.when(step == pl.num_programs(0) - 1)
    def _():
        out_ref[...] = total[...].astype(jnp.bfloat16)


def weight_kernel(mask_ref, turned_ref, grads_ref, out_ref):
    for block in range(mask_ref.shape[0]):
        rows = pl.ds(block * TILE, TILE)
        product = jnp.dot(
            turned_ref[rows, :], grads_ref[...], preferred_element_type=jnp.float32
        )
        live = jnp.broadcast_to(mask_ref[block : block + 1, :], product.shape) > 0.5
        out_ref[rows, :] = jnp.where(live, product, 0.0).astype(jnp.bfloat16)


def run(kernel, mask, left, right, width, left_blocked, out, out_blocked, scratch):
    blocks, total_width = mask.shape
    depth = blocks * TILE
    column = lambda rows: pl.BlockSpec((rows, width), lambda i: (0, i))
    whole = lambda shape: pl.BlockSpec(shape, lambda i: (0, 0))
    moved = sum(a.size * a.dtype.itemsize for a in (left, right)) + out[0] * out[1] * 2
    count = left.shape[1] if kernel is weight_kernel else left.shape[0]
    return pl.pallas_call(
        kernel,
        grid=(total_width // width,),
        in_specs=[
            column(blocks),
            column(left.shape[0]) if left_blocked else whole(left.shape),
            column(right.shape[0]),
        ],
        out_specs=column(out[0]) if out_blocked else whole(out),
        out_shape=jax.ShapeDtypeStruct(out, jnp.bfloat16),
        scratch_shapes=scratch,
        cost_estimate=pl.CostEstimate(
            flops=2 * count * depth * total_width, bytes_accessed=moved, transcendentals=0
        ),
        compiler_params=pltpu.CompilerParams(
            dimension_semantics=("arbitrary",), vmem_limit_bytes=48 * 1024 * 1024
        ),
    )(mask, left, right)


def on_device(tokens, weight, tile_rows, tile_cols, tile_count, hidden_cotangent):
    row_index = lax.axis_index("row")
    col_index = lax.axis_index("col")
    row_blocks = weight.shape[0] // TILE
    col_blocks = weight.shape[1] // TILE
    capacity = tile_rows.shape[2]
    local_rows = tile_rows.reshape(capacity) - col_index * row_blocks
    local_cols = tile_cols.reshape(capacity) - row_index * col_blocks
    is_live = jnp.arange(capacity) < tile_count.reshape(())
    row_pick = (
        (local_rows[None, :] == jnp.arange(row_blocks)[:, None]) & is_live[None, :]
    ).astype(jnp.bfloat16)
    col_pick = (local_cols[:, None] == (jnp.arange(weight.shape[1]) // TILE)[None, :]).astype(
        jnp.bfloat16
    )
    mask = jnp.dot(row_pick, col_pick, preferred_element_type=jnp.float32)
    width = min(512, weight.shape[1])
    held = pltpu.VMEM((weight.shape[0], width), jnp.bfloat16)

    full_tokens = lax.all_gather(tokens, "row", axis=0, tiled=True)
    count = full_tokens.shape[0]
    partial = run(
        forward_kernel, mask, full_tokens, weight, width, False,
        (count, weight.shape[1]), True, [held],
    )
    pre_act = paired_exchange_sum(partial, "col")
    gate_value = jax.nn.sigmoid(pre_act)
    hidden = (pre_act * gate_value).astype(jnp.bfloat16)
    silu_slope = gate_value * (1.0 + pre_act * (1.0 - gate_value))
    grad_pre = (hidden_cotangent.astype(jnp.float32) * silu_slope).astype(jnp.bfloat16)
    full_grads = lax.all_gather(grad_pre, "col", axis=0, tiled=True)
    share_shape = (count, weight.shape[0])
    share = run(
        backward_kernel, mask, full_grads, weight, width, True,
        share_shape, False, [held, pltpu.VMEM(share_shape, jnp.float32)],
    )
    input_grad = exchange_sum(share, "row").astype(jnp.bfloat16)
    weight_grad = run(
        weight_kernel, mask, full_tokens.T, full_grads, width, False,
        weight.shape, True, [],
    )
    return (hidden, input_grad, weight_grad)


def solution(mesh):
    in_specs = (
        P("row", "col"),
        P("col", "row"),
        P("row", "col", None),
        P("row", "col", None),
        P("row", "col"),
        P("col", "row"),
    )
    out_specs = (P("col", "row"), P("row", "col"), P("col", "row"))
    return jax.shard_map(
        on_device, mesh=mesh, in_specs=in_specs, out_specs=out_specs, check_vma=False
    )
```
